32 devices in a mesh: group: 2 (over x), expert: 16 (over z, y, core).
Axes of the slice: x: 2, y: 2, z: 4, core: 2. Of those that a mesh axis runs over, the one named last changes fastest.
Arguments:
- tokens: bfloat16 [4096, 4096], P(('group', 'expert')), parts along dimension 0, may hold values from -6 to 6
- expert_ids: int32 [4096, 8], P(('group', 'expert')), parts along dimension 0, may hold values from 0 to 15, all different within a row; in each aligned block of 128 rows (0 to 127, 128 to 255, ...) at most 72 rows name the same one
- gate_weights: float32 [4096, 8], P(('group', 'expert')), parts along dimension 0, may hold values from 0.05 to 0.25
- weights_in: bfloat16 [32, 4096, 1536], P(('group', 'expert')), parts along dimension 0, may hold values from -0.09375 to 0.09375
- weights_out: bfloat16 [32, 768, 4096], P(('group', 'expert')), parts along dimension 0, may hold values from -0.21875 to 0.21875
- placement: int32 [32], P('group'), parts along dimension 0, may hold values from 0 to 15, each once
- capacity: int32 [32], P('group'), parts along dimension 0, may hold values from 691 to 1152, as said below
Outputs:
- moe_out: bfloat16 [4096, 4096], P(('group', 'expert')), parts along dimension 0
The draws below stay inside these ranges and needn't reach their ends.
There are 2 independent parts, one for each index of `group`. The reference program is written for one: setup_inputs(seed, part) draws one part's arguments, and reference() takes and returns one part's arrays. A program takes and returns all parts, laid end to end along the dimension named above; each array names one. Nothing has to cross between parts.
Inputs may be any that keep to these rules, and one draw needn't show every extreme that they name: `expert_ids`: each row names 8 different experts; among the rows of one device no expert is named by more than 72 rows, and that bound is reached in every draw. `placement`: A permutation of the experts. The largest capacity equals 1152 in every draw.
All inputs are finite; a program needn't handle non-finite values.
Results may differ from the reference program's by a relative error of at most 0.0058.
Values may be sent and summed in bfloat16 or wider, within the bound.
No kernel may reach another device: no remote copies, remote signals or barrier semaphores. Data moves between devices by JAX's collectives and lax.ppermute only.
A program may use at most 128 MiB of HBM per device.

```python
import math
import jax
import jax.numpy as jnp
import numpy as np
from jax import lax

D = 4096
TOP = 8
FFW = 768
TOK_DEV = 128
EXPERTS = 16
TOKENS = 2048
SLOT = 72
CAP_HI = 1152
CAP_LO = 691


def draw_capacity(key, part):
    key_values, key_top = jax.random.split(key)
    values = jax.random.randint(key_values, (EXPERTS,), CAP_LO, CAP_HI + 1)
    top_slot = jax.random.randint(key_top, (), 0, EXPERTS)
    return jnp.where(jnp.arange(EXPERTS) == top_slot, CAP_HI, values).astype(jnp.int32)


def block_levels(key, shape, pieces, smallest, top_value):
    loudness = 1.0
    for axis_at, blocks in pieces:
        draws = jax.random.uniform(jax.random.fold_in(jax.random.fold_in(key, 6), axis_at), (blocks,), jnp.float32, smallest / len(pieces), top_value / len(pieces))
        loudness = loudness * jnp.repeat(jnp.exp(draws), shape[axis_at] // blocks).reshape((-1,) + (1,) * (len(shape) - 1 - axis_at))
    return loudness


def shared_out(rng, own, number, rows, count, top, bound, lean):
    sequence = jax.random.permutation(rng, count)
    packed, ordinary = portions_of(count, rows * top, bound, lean, True), portions_of(count, rows * top, bound, lean, False)
    places = jnp.arange(count)

    def named(tallies, turn):
        used = int((tallies > 0).sum())
        fixed = max(1, used // 4)
        passed = fixed + (places - fixed + turn * (used - fixed)) % max(1, count - fixed)
        return jnp.zeros((count,), jnp.int32).at[sequence[jnp.where(places < fixed, places, passed)]].set(jnp.asarray(tallies, jnp.int32))

    tallies = jnp.where(number % 4 == 0, named(packed, number // 4), named(ordinary, number - number // 4 - 1))
    mixed = jax.random.permutation(jax.random.fold_in(own, 3), count)
    donor, sink = mixed[0:count // 2 * 2:2], mixed[1:count // 2 * 2:2]
    room = jnp.minimum(tallies[donor] - 1, bound - tallies[sink]) // 2
    room = jnp.where((donor == sequence[0]) | (sink == sequence[0]) | (tallies[sink] == 0), 0, jnp.maximum(room, 0))
    passed = jax.random.randint(jax.random.fold_in(own, 4), (count // 2,), 0, 1 << 20) % (room + 1)
    tallies = tallies.at[donor].add(-passed).at[sink].add(passed)
    members = jnp.searchsorted(jnp.cumsum(tallies), jnp.arange(rows * top), side="right").astype(jnp.int32)
    grid = members.reshape(top, rows).T
    grid = grid[jax.random.permutation(jax.random.fold_in(own, 1), rows)]
    turn = jax.random.randint(jax.random.fold_in(own, 2), (rows, 1), 0, top)
    return jnp.take_along_axis(grid, (jnp.arange(top)[None, :] + turn) % top, axis=1)


def portions_of(number_of, total, reach, slope, full):
    weights = [(1 << 20) // math.isqrt(grade ** slope) + 1 for grade in range(1, number_of + 1)]
    largest = reach if full else min(reach, max(-(-total // number_of), total * weights[0] // sum(weights)))
    least = 1 if total - largest >= number_of - 1 else 0
    holding, spare = [largest] + [least] * (number_of - 1), total - largest - least * (number_of - 1)
    while spare > 0:
        free = [i for i in range(1, number_of) if holding[i] < largest] or [i for i in range(1, number_of) if holding[i] < reach]
        whole, left = sum([weights[i] for i in free]), spare
        for i in free:
            extra = min(reach - holding[i], max(1, left * weights[i] // whole), spare)
            holding[i] = holding[i] + extra
            spare = spare - extra
    return np.array(holding)


def scatter_about(own_key, extent, scale, reach, cuts=(), kind=jnp.bfloat16):
    gain = block_levels(own_key, extent, cuts, -0.22, 0.18) if cuts else 1.0
    array = jax.random.normal(own_key, extent, jnp.float32) * scale * gain
    return jnp.minimum(jnp.maximum(array, -reach), reach).astype(kind)


def setup_inputs(seed: int = 0, part: int = 0) -> dict:
    key_list = jax.random.split(jax.random.key(seed), 8)
    part_splits = jax.random.split(jax.random.fold_in(key_list[7], part), 8)
    tokens = scatter_about(part_splits[0], (TOKENS, D), 1.0, 6.0, ((0, 16),))
    expert_ids_keys = jax.random.split(jax.random.fold_in(part_splits[1], 1), TOKENS // TOK_DEV)
    expert_ids_turns = jax.random.permutation(jax.random.fold_in(part_splits[1], 3), TOKENS // TOK_DEV)
    expert_ids = jax.vmap(lambda own, number: shared_out(jax.random.fold_in(part_splits[1], 2), own, number, TOK_DEV, EXPERTS, TOP, SLOT, 2))(expert_ids_keys, expert_ids_turns).reshape((TOKENS, TOP))
    gate_weights = jnp.clip(0.05 + 0.2 * jax.random.uniform(part_splits[2], (TOKENS, TOP), jnp.float32) ** block_levels(part_splits[2], (TOKENS, TOP), ((0, 16),), -0.2, 0.2), 0.05, 0.25)
    weights_in = scatter_about(part_splits[3], (EXPERTS, D, 2 * FFW), D ** -0.5, 0.09375, ((0, 16),))
    weights_out = scatter_about(part_splits[4], (EXPERTS, FFW, D), FFW ** -0.5, 0.21875, ((0, 16),))
    placement = jax.random.permutation(part_splits[5], EXPERTS).astype(jnp.int32)
    capacity = draw_capacity(jax.random.fold_in(jax.random.fold_in(key_list[7], part), 71), part)
    return dict(tokens=tokens, expert_ids=expert_ids, gate_weights=gate_weights, weights_in=weights_in, weights_out=weights_out, placement=placement, capacity=capacity)


def expert_rows(inputs, first_weights, second_weights):
    projected = jnp.dot(inputs, first_weights, preferred_element_type=jnp.float32)
    gate_part = projected[:, :FFW]
    up_part = projected[:, FFW:]
    hidden = (jax.nn.silu(gate_part) * up_part).astype(jnp.bfloat16)
    return jnp.dot(hidden, second_weights, preferred_element_type=jnp.float32).astype(jnp.bfloat16)


def reference(tokens, expert_ids, gate_weights, weights_in, weights_out, placement, capacity):
    devices = jnp.arange(EXPERTS, dtype=jnp.int32)
    dev_of = jnp.zeros((EXPERTS,), jnp.int32).at[placement].set(devices)
    flat_ids = expert_ids.reshape(-1)
    onehot = (flat_ids[:, None] == devices[None, :]).astype(jnp.int32)
    before = jnp.cumsum(onehot, axis=0) - onehot
    rank = jnp.sum(before * onehot, axis=1)
    kept = rank < capacity[flat_ids]
    flat_gates = gate_weights.reshape(-1)

    def one_expert(running, expert):
        chosen = (flat_ids == expert) & kept
        picked = jnp.nonzero(chosen, size=CAP_HI, fill_value=0)[0].astype(jnp.int32)
        live = jnp.arange(CAP_HI) < jnp.sum(chosen.astype(jnp.int32))
        block_idx = dev_of[expert]
        token_idx = (picked // TOP).astype(jnp.int32)
        outputs_rows = expert_rows(tokens[token_idx], weights_in[block_idx], weights_out[block_idx])
        term = jnp.where(live[:, None], flat_gates[picked][:, None] * outputs_rows.astype(jnp.float32), jnp.float32(0.0))
        return running.at[token_idx].add(term), None

    start = jnp.zeros((TOKENS, D), jnp.float32)
    running, _ = lax.scan(one_expert, start, devices)
    return running.astype(jnp.bfloat16)
```

```python
import jax
import jax.numpy as jnp
from jax import lax
from jax.sharding import PartitionSpec as P

AXIS = "expert"


def expert_block(inputs, first_weights, second_weights):
    hidden_len = first_weights.shape[1] // 2
    projected = jnp.dot(inputs, first_weights, preferred_element_type=jnp.float32)
    gate_part = projected[:, :hidden_len]
    up_part = projected[:, hidden_len:]
    hidden = (jax.nn.silu(gate_part) * up_part).astype(jnp.bfloat16)
    return jnp.dot(hidden, second_weights, preferred_element_type=jnp.float32).astype(jnp.bfloat16)


def row_weights(expert_ids, gate_weights, placement, capacity):
    axis_len = lax.axis_size(AXIS)
    rows = expert_ids.shape[0]
    top_len = expert_ids.shape[1]
    mine = lax.axis_index(AXIS)
    expert = lax.dynamic_index_in_dim(placement, mine, 0, False)
    limit = lax.dynamic_index_in_dim(capacity, expert, 0, False)
    packed = jnp.concatenate([expert_ids.T.astype(jnp.float32), gate_weights.T], axis=0)
    everyone = lax.all_gather(packed, AXIS)
    named = everyone[:, :top_len] == expert.astype(jnp.float32)
    gate = jnp.sum(jnp.where(named, everyone[:, top_len:], 0.0), axis=1)
    hit = jnp.sum(named.astype(jnp.float32), axis=1)
    lower = jnp.arange(rows)[:, None] < jnp.arange(rows)[None, :]
    within = jnp.dot(hit, lower.astype(jnp.float32), precision=lax.Precision.HIGHEST)
    total = jnp.sum(hit, axis=1)
    earlier = jnp.arange(axis_len)[None, :] < jnp.arange(axis_len)[:, None]
    ahead = jnp.sum(jnp.where(earlier, total[None, :], 0.0), axis=1)
    rank = within + ahead[:, None]
    return jnp.where((hit > 0) & (rank < limit.astype(jnp.float32)), gate, 0.0)


def ring_form(tokens, expert_ids, gate_weights, weights_in, weights_out, placement, capacity):
    axis_len = lax.axis_size(AXIS)
    rows, feat_len = tokens.shape
    half = rows // 2
    chips = axis_len // 2
    side = chips // 2

    def chip_at(spot):
        return 2 * spot if spot < side else 2 * (chips - 1 - spot) + 1

    spot_of = {chip_at(spot): spot for spot in range(chips)}

    def along(step):
        return [(d, 2 * chip_at((spot_of[d // 2] + step) % chips) + d % 2) for d in range(axis_len)]

    forth, back = along(1), along(-1)
    swap = [(d, d ^ 1) for d in range(axis_len)]

    table = row_weights(expert_ids, gate_weights, placement, capacity).reshape(axis_len, 2, half, 1)
    mine = lax.axis_index(AXIS)
    chip, core = mine // 2, mine % 2
    spot = jnp.where(chip % 2 == 0, chip // 2, chips - 1 - chip // 2)

    def weight_of(place, which_core, part):
        place = lax.rem(place + chips, chips)
        its_chip = jnp.where(place < side, 2 * place, 2 * (chips - 1 - place) + 1)
        return lax.dynamic_index_in_dim(table, 2 * its_chip + which_core, 0, False)[part]

    first_weights, second_weights = weights_in[0], weights_out[0]
    ahead, behind = tokens[:half], tokens[half:]
    own_parts = []
    for step in range(chips):
        if step:
            ahead = lax.ppermute(ahead, AXIS, forth)
            behind = lax.ppermute(behind, AXIS, back)
        own = tokens if step == 0 else jnp.concatenate([ahead, behind], axis=0)
        other = lax.ppermute(own, AXIS, swap)
        outs = expert_block(jnp.concatenate([own, other], axis=0), first_weights, second_weights)
        scale = jnp.concatenate(
            [
                weight_of(spot - step, core, 0),
                weight_of(spot + step, core, 1),
                weight_of(spot - step, 1 - core, 0),
                weight_of(spot + step, 1 - core, 1),
            ],
            axis=0,
        )
        scaled = outs.astype(jnp.float32) * scale
        from_other = lax.ppermute(scaled[rows:].astype(jnp.bfloat16), AXIS, swap)
        own_parts.append((scaled[:rows], from_other))
        if step == 1:
            sums = scaled[:rows] + from_other.astype(jnp.float32)
            sums_a, sums_b = sums[:half].astype(jnp.bfloat16), sums[half:].astype(jnp.bfloat16)
        elif step > 1:
            mine_part = scaled[:rows] + from_other.astype(jnp.float32)
            got_a = lax.ppermute(sums_a, AXIS, forth).astype(jnp.float32)
            got_b = lax.ppermute(sums_b, AXIS, back).astype(jnp.float32)
            sums_a = (got_a + mine_part[:half]).astype(jnp.bfloat16)
            sums_b = (got_b + mine_part[half:]).astype(jnp.bfloat16)
    first_scaled, first_other = own_parts[0]
    mine_part = first_scaled + first_other.astype(jnp.float32)
    got_a = lax.ppermute(sums_a, AXIS, forth).astype(jnp.float32)
    got_b = lax.ppermute(sums_b, AXIS, back).astype(jnp.float32)
    result = jnp.concatenate([got_a + mine_part[:half], got_b + mine_part[half:]], axis=0)
    return result.astype(jnp.bfloat16)


def prefix(part):
    gathered = lax.all_gather(part, AXIS)
    earlier = jnp.arange(gathered.shape[0]) < lax.axis_index(AXIS)
    return jnp.sum(jnp.where(earlier[:, None], gathered, 0), axis=0)


def exchange_form(tokens, expert_ids, gate_weights, weights_in, weights_out, placement, capacity):
    axis_len = lax.axis_size(AXIS)
    tok_rows, top_len = expert_ids.shape
    feat_len = tokens.shape[1]
    slot_len = tok_rows * top_len * 9 // (8 * axis_len)
    devices = jnp.arange(axis_len, dtype=jnp.int32)
    dev_of = jnp.sum(jnp.where(placement[:, None] == devices[None, :], devices[:, None], 0), axis=0)
    flat_ids = expert_ids.reshape(-1)
    onehot = (flat_ids[:, None] == devices[None, :]).astype(jnp.int32)
    before = jnp.cumsum(onehot, axis=0) - onehot
    local_rank = jnp.sum(before * onehot, axis=1)
    counts = jnp.sum(onehot, axis=0)
    offset = prefix(counts)
    row_offset = jnp.sum(onehot * offset[None, :], axis=1)
    row_cap = jnp.sum(onehot * capacity[None, :], axis=1)
    row_dest = jnp.sum(onehot * dev_of[None, :], axis=1)
    kept = local_rank + row_offset < row_cap
    flat_slot = row_dest * slot_len + local_rank
    row_token = jnp.arange(tok_rows * top_len, dtype=jnp.int32) // top_len
    owner = jnp.full((axis_len * slot_len,), tok_rows, jnp.int32).at[flat_slot].set(row_token)
    padded_tokens = jnp.concatenate([tokens, jnp.zeros((1, feat_len), jnp.bfloat16)], axis=0)
    outgoing = padded_tokens[owner].reshape(axis_len, slot_len, feat_len)
    arrived = lax.all_to_all(outgoing, AXIS, split_axis=0, concat_axis=0, tiled=True)
    items = arrived.shape[1]
    result_rows = expert_block(
        arrived.reshape(axis_len * items, feat_len), weights_in[0], weights_out[0]
    )
    result_rows = result_rows.reshape(axis_len, items, feat_len)
    returned = lax.all_to_all(result_rows, AXIS, split_axis=0, concat_axis=0, tiled=True)
    picked = returned.reshape(axis_len * slot_len, feat_len)[flat_slot]
    row_weight = jnp.where(kept, gate_weights.reshape(-1), jnp.float32(0.0))
    combined = jnp.sum(
        (row_weight[:, None] * picked.astype(jnp.float32)).reshape(tok_rows, top_len, feat_len),
        axis=1,
    )
    return combined.astype(jnp.bfloat16)


def local(*args):
    axis_len, top_len = lax.axis_size(AXIS), args[1].shape[1]
    dense = axis_len <= 2 * top_len and axis_len % 4 == 0
    return ring_form(*args) if dense else exchange_form(*args)


def solution(mesh):
    in_specs = (
        P(("group", "expert"), None),
        P(("group", "expert"), None),
        P(("group", "expert"), None),
        P(("group", "expert"), None, None),
        P(("group", "expert"), None, None),
        P("group"),
        P("group"),
    )
    out_specs = P(("group", "expert"), None)
    return jax.shard_map(local, mesh=mesh, in_specs=in_specs, out_specs=out_specs, check_vma=False)
```

```python
import jax
import jax.numpy as jnp
import numpy as np
from jax import lax
from jax.experimental import pallas as pl
from jax.experimental.pallas import tpu as pltpu
from jax.sharding import PartitionSpec as P

AXIS = "expert"
COST = pl.CostEstimate(flops=12_000_000_000, transcendentals=0, bytes_accessed=60_000_000)


def expert_block(inputs, first_weights, second_weights):
    hidden_len = first_weights.shape[1] // 2
    projected = jnp.dot(inputs, first_weights, preferred_element_type=jnp.float32)
    gate_part = projected[:, :hidden_len]
    up_part = projected[:, hidden_len:]
    hidden = (jax.nn.silu(gate_part) * up_part).astype(jnp.bfloat16)
    return jnp.dot(hidden, second_weights, preferred_element_type=jnp.float32).astype(jnp.bfloat16)


def incoming_gates(expert_ids, gate_weights, placement):
    named = expert_ids.T[None] == placement[:, None, None]
    outgoing = jnp.sum(jnp.where(named, gate_weights.T[None], 0.0), axis=1)
    return lax.all_to_all(outgoing[:, None], AXIS, split_axis=0, concat_axis=0, tiled=True)[:, 0]


def table_kernel(limit, where, gate_ref, *refs):
    gate = gate_ref[...]
    devices, rows = gate.shape
    hit = jnp.where(gate > 0, 1.0, 0.0).astype(jnp.bfloat16)
    shape = (rows, rows)
    lower = lax.broadcasted_iota(jnp.int32, shape, 0) < lax.broadcasted_iota(jnp.int32, shape, 1)
    lower = jnp.where(lower, 1.0, 0.0).astype(jnp.bfloat16)
    within = jnp.dot(hit, lower, preferred_element_type=jnp.float32)
    shape = (devices, devices)
    earlier = lax.broadcasted_iota(jnp.int32, shape, 1) < lax.broadcasted_iota(jnp.int32, shape, 0)
    earlier = jnp.where(earlier, 1.0, 0.0).astype(jnp.bfloat16)
    before = jnp.dot(earlier, hit, preferred_element_type=jnp.float32)
    rank = within + jnp.sum(before, axis=1, keepdims=True)
    table = jnp.where(rank < limit[0].astype(jnp.float32), gate, 0.0).T
    out = refs[-1]
    steps = out.shape[1]
    half = rows // 2
    column = lax.broadcasted_iota(jnp.int32, (half, devices), 1)
    turn = lax.broadcasted_iota(jnp.int32, (half, steps), 1)
    for index in range(4):
        part = index % 2 * half
        piece = table[part : part + half]
        made = jnp.zeros((half, steps), jnp.float32)
        for step in range(steps):
            picked = jnp.sum(jnp.where(column == where[step, index], piece, 0.0), axis=1, keepdims=True)
            made = jnp.where(turn == step, picked, made)
        out[index * half : (index + 1) * half, :] = made


def weight_table(gate, where, placement, capacity, gates):
    expert = lax.dynamic_index_in_dim(placement, lax.axis_index(AXIS), 0, False)
    limit = lax.dynamic_index_in_dim(capacity, expert, 0, True)
    smem = pl.BlockSpec(memory_space=pltpu.SMEM)
    hbm = pl.BlockSpec(memory_space=pl.ANY)
    vmem = pl.BlockSpec(memory_space=pltpu.VMEM)
    return pl.pallas_call(
        table_kernel,
        out_shape=jax.ShapeDtypeStruct((2 * gate.shape[1], where.shape[0]), jnp.float32),
        in_specs=[smem, smem, vmem] + [hbm] * len(gates),
        out_specs=vmem,
        cost_estimate=COST,
    )(limit, where, gate, *gates)


def ring_form(tokens, expert_ids, gate_weights, weights_in, weights_out, placement, capacity):
    axis_len = lax.axis_size(AXIS)
    rows = tokens.shape[0]
    half = rows // 2
    chips = axis_len // 2
    side = chips // 2

    def chip_at(spot):
        return 2 * spot if spot < side else 2 * (chips - 1 - spot) + 1

    spot_of = {chip_at(spot): spot for spot in range(chips)}

    def along(step):
        return [(d, 2 * chip_at((spot_of[d // 2] + step) % chips) + d % 2) for d in range(axis_len)]

    forth, back = along(1), along(-1)
    swap = [(d, d ^ 1) for d in range(axis_len)]

    def send(value, where, name):
        with jax.named_scope(name):
            return lax.ppermute(value, AXIS, where)

    owners = np.zeros((axis_len, chips, 4), np.int32)
    for d in range(axis_len):
        for step in range(chips):
            for index, (way, core) in enumerate([(-1, 0), (1, 0), (-1, 1), (1, 1)]):
                owners[d, step, index] = 2 * chip_at((spot_of[d // 2] + way * step) % chips) + (d + core) % 2
    where = lax.dynamic_index_in_dim(jnp.asarray(owners), lax.axis_index(AXIS), 0, False)
    first_weights, second_weights = weights_in[0], weights_out[0]

    aheads, behinds = [tokens[:half]], [tokens[half:]]
    for step in range(1, chips):
        aheads.append(send(aheads[-1], forth, f"ag{step}a"))
        behinds.append(send(behinds[-1], back, f"ag{step}b"))
    with jax.named_scope("meta"):
        gate = incoming_gates(expert_ids, gate_weights, placement)
        scales = weight_table(gate, where, placement, capacity, (aheads[1], behinds[1]))
    sums_a = sums_b = None
    for turn in range(1, chips + 1):
        step = turn % chips
        pieces = [aheads[step], behinds[step]]
        pieces += [send(pieces[0], swap, f"xs{step}a"), send(pieces[1], swap, f"xs{step}b")]
        with jax.named_scope(f"kernel{step}"):
            outs = expert_block(jnp.concatenate(pieces, axis=0), first_weights, second_weights)
            outs = outs.astype(jnp.float32) * scales[:, step : step + 1]
            kept, other = outs[:rows], outs[rows:].astype(jnp.bfloat16)
        from_other = send(other, swap, f"ps{step}")
        with jax.named_scope(f"add{step}"):
            part = kept + from_other.astype(jnp.float32)
            part_a, part_b = part[:half], part[half:]
        if turn != 1:
            sums_a, sums_b = send(sums_a, forth, f"rs{step}a"), send(sums_b, back, f"rs{step}b")
            with jax.named_scope(f"add{step}"):
                part_a, part_b = part_a + sums_a.astype(jnp.float32), part_b + sums_b.astype(jnp.float32)
        with jax.named_scope(f"add{step}"):
            sums_a, sums_b = part_a.astype(jnp.bfloat16), part_b.astype(jnp.bfloat16)
    return jnp.concatenate([sums_a, sums_b], axis=0)


def prefix(part):
    gathered = lax.all_gather(part, AXIS)
    earlier = jnp.arange(gathered.shape[0]) < lax.axis_index(AXIS)
    return jnp.sum(jnp.where(earlier[:, None], gathered, 0), axis=0)


def exchange_form(tokens, expert_ids, gate_weights, weights_in, weights_out, placement, capacity):
    axis_len = lax.axis_size(AXIS)
    tok_rows, top_len = expert_ids.shape
    feat_len = tokens.shape[1]
    slot_len = tok_rows * top_len * 9 // (8 * axis_len)
    devices = jnp.arange(axis_len, dtype=jnp.int32)
    dev_of = jnp.sum(jnp.where(placement[:, None] == devices[None, :], devices[:, None], 0), axis=0)
    flat_ids = expert_ids.reshape(-1)
    onehot = (flat_ids[:, None] == devices[None, :]).astype(jnp.int32)
    before = jnp.cumsum(onehot, axis=0) - onehot
    local_rank = jnp.sum(before * onehot, axis=1)
    counts = jnp.sum(onehot, axis=0)
    offset = prefix(counts)
    row_offset = jnp.sum(onehot * offset[None, :], axis=1)
    row_cap = jnp.sum(onehot * capacity[None, :], axis=1)
    row_dest = jnp.sum(onehot * dev_of[None, :], axis=1)
    kept = local_rank + row_offset < row_cap
    flat_slot = row_dest * slot_len + local_rank
    row_token = jnp.arange(tok_rows * top_len, dtype=jnp.int32) // top_len
    owner = jnp.full((axis_len * slot_len,), tok_rows, jnp.int32).at[flat_slot].set(row_token)
    padded_tokens = jnp.concatenate([tokens, jnp.zeros((1, feat_len), jnp.bfloat16)], axis=0)
    outgoing = padded_tokens[owner].reshape(axis_len, slot_len, feat_len)
    arrived = lax.all_to_all(outgoing, AXIS, split_axis=0, concat_axis=0, tiled=True)
    items = arrived.shape[1]
    result_rows = expert_block(
        arrived.reshape(axis_len * items, feat_len), weights_in[0], weights_out[0]
    )
    result_rows = result_rows.reshape(axis_len, items, feat_len)
    returned = lax.all_to_all(result_rows, AXIS, split_axis=0, concat_axis=0, tiled=True)
    picked = returned.reshape(axis_len * slot_len, feat_len)[flat_slot]
    row_weight = jnp.where(kept, gate_weights.reshape(-1), jnp.float32(0.0))
    combined = jnp.sum(
        (row_weight[:, None] * picked.astype(jnp.float32)).reshape(tok_rows, top_len, feat_len),
        axis=1,
    )
    return combined.astype(jnp.bfloat16)


def local(*args):
    axis_len, top_len = lax.axis_size(AXIS), args[1].shape[1]
    dense = axis_len <= 2 * top_len and axis_len % 4 == 0
    return ring_form(*args) if dense else exchange_form(*args)


def solution(mesh):
    in_specs = (
        P(("group", "expert"), None),
        P(("group", "expert"), None),
        P(("group", "expert"), None),
        P(("group", "expert"), None, None),
        P(("group", "expert"), None, None),
        P("group"),
        P("group"),
    )
    out_specs = P(("group", "expert"), None)
    return jax.shard_map(local, mesh=mesh, in_specs=in_specs, out_specs=out_specs, check_vma=False)
```

```python
import jax
import jax.numpy as jnp
import numpy as np
from jax import lax
from jax.experimental import pallas as pl
from jax.experimental.pallas import tpu as pltpu
from jax.sharding import PartitionSpec as P

AXIS = "expert"
COST = pl.CostEstimate(flops=12_000_000_000, transcendentals=0, bytes_accessed=60_000_000)


def expert_block(inputs, first_weights, second_weights):
    hidden_len = first_weights.shape[1] // 2
    projected = jnp.dot(inputs, first_weights, preferred_element_type=jnp.float32)
    gate_part = projected[:, :hidden_len]
    up_part = projected[:, hidden_len:]
    hidden = (jax.nn.silu(gate_part) * up_part).astype(jnp.bfloat16)
    return jnp.dot(hidden, second_weights, preferred_element_type=jnp.float32).astype(jnp.bfloat16)


def incoming_gates(expert_ids, gate_weights, placement):
    named = expert_ids.T[None] == placement[:, None, None]
    outgoing = jnp.sum(jnp.where(named, gate_weights.T[None], 0.0), axis=1)
    return lax.all_to_all(outgoing[:, None], AXIS, split_axis=0, concat_axis=0, tiled=True)[:, 0]


def table_kernel(mine, placement, capacity, owners, gate_ref, *refs):
    limit = capacity[placement[mine[0]]]
    gate = gate_ref[...]
    devices, rows = gate.shape
    hit = jnp.where(gate > 0, 1.0, 0.0).astype(jnp.bfloat16)
    shape = (rows, rows)
    lower = lax.broadcasted_iota(jnp.int32, shape, 0) < lax.broadcasted_iota(jnp.int32, shape, 1)
    lower = jnp.where(lower, 1.0, 0.0).astype(jnp.bfloat16)
    within = jnp.dot(hit, lower, preferred_element_type=jnp.float32)
    shape = (devices, devices)
    earlier = lax.broadcasted_iota(jnp.int32, shape, 1) < lax.broadcasted_iota(jnp.int32, shape, 0)
    earlier = jnp.where(earlier, 1.0, 0.0).astype(jnp.bfloat16)
    before = jnp.dot(earlier, hit, preferred_element_type=jnp.float32)
    rank = within + jnp.sum(before, axis=1, keepdims=True)
    table = jnp.where(rank < limit.astype(jnp.float32), gate, 0.0).T
    out = refs[-1]
    steps = out.shape[1]
    half = rows // 2
    column = lax.broadcasted_iota(jnp.int32, (half, devices), 1)
    turn = lax.broadcasted_iota(jnp.int32, (half, steps), 1)
    for index in range(4):
        part = index % 2 * half
        piece = table[part : part + half]
        made = jnp.zeros((half, steps), jnp.float32)
        for step in range(steps):
            picked = jnp.sum(jnp.where(column == owners[(mine[0] * steps + step) * 4 + index], piece, 0.0), axis=1, keepdims=True)
            made = jnp.where(turn == step, picked, made)
        out[index * half : (index + 1) * half, :] = made


def weight_table(gate, owners, placement, capacity, gates):
    smem = pl.BlockSpec(memory_space=pltpu.SMEM)
    hbm = pl.BlockSpec(memory_space=pl.ANY)
    vmem = pl.BlockSpec(memory_space=pltpu.VMEM)
    mine = lax.axis_index(AXIS).astype(jnp.int32).reshape(1)
    return pl.pallas_call(
        table_kernel,
        out_shape=jax.ShapeDtypeStruct((2 * gate.shape[1], owners.shape[1]), jnp.float32),
        in_specs=[smem] * 4 + [vmem] + [hbm] * len(gates),
        out_specs=vmem,
        cost_estimate=COST,
    )(mine, placement, capacity, jnp.asarray(owners.reshape(-1)), gate, *gates)


def ring_form(tokens, expert_ids, gate_weights, weights_in, weights_out, placement, capacity):
    axis_len = lax.axis_size(AXIS)
    rows = tokens.shape[0]
    half = rows // 2
    chips = axis_len // 2
    side = chips // 2

    def chip_at(spot):
        return 2 * spot if spot < side else 2 * (chips - 1 - spot) + 1

    spot_of = {chip_at(spot): spot for spot in range(chips)}

    def along(step):
        return [(d, 2 * chip_at((spot_of[d // 2] + step) % chips) + d % 2) for d in range(axis_len)]

    forth, back = along(1), along(-1)
    swap = [(d, d ^ 1) for d in range(axis_len)]

    def send(value, where, name):
        with jax.named_scope(name):
            return lax.ppermute(value, AXIS, where)

    owners = np.zeros((axis_len, chips, 4), np.int32)
    for d in range(axis_len):
        for step in range(chips):
            for index, (way, core) in enumerate([(-1, 0), (1, 0), (-1, 1), (1, 1)]):
                owners[d, step, index] = 2 * chip_at((spot_of[d // 2] + way * step) % chips) + (d + core) % 2
    first_weights, second_weights = weights_in[0], weights_out[0]

    aheads, behinds = [tokens[:half]], [tokens[half:]]
    for step in range(1, chips):
        aheads.append(send(aheads[-1], forth, f"ag{step}a"))
        behinds.append(send(behinds[-1], back, f"ag{step}b"))
    with jax.named_scope("meta"):
        gate = incoming_gates(expert_ids, gate_weights, placement)
        scales = weight_table(gate, owners, placement, capacity, (aheads[1], behinds[1]))
    joined = min(3, chips - 1)
    sums_a = sums_b = None
    for turn in range(1, chips + 1):
        step = turn % chips
        pieces = [aheads[step], behinds[step]]
        if step:
            pieces += [send(pieces[0], swap, f"xs{step}a"), send(pieces[1], swap, f"xs{step}b")]
        with jax.named_scope(f"kernel{step}"):
            if step == joined:
                pieces += [tokens, send(tokens, swap, "xs0")]
            if step:
                outs = expert_block(jnp.concatenate(pieces, axis=0), first_weights, second_weights)
            else:
                outs = own_outs
            if step == joined:
                outs, own_outs = outs[: 2 * rows], outs[2 * rows :]
            outs = outs.astype(jnp.float32) * scales[:, step : step + 1]
            kept, other = outs[:rows], outs[rows:].astype(jnp.bfloat16)
        from_other = send(other, swap, f"ps{step}")
        with jax.named_scope(f"add{step}"):
            part = kept + from_other.astype(jnp.float32)
            part_a, part_b = part[:half], part[half:]
        if turn != 1:
            sums_a, sums_b = send(sums_a, forth, f"rs{step}a"), send(sums_b, back, f"rs{step}b")
            with jax.named_scope(f"add{step}"):
                part_a, part_b = part_a + sums_a.astype(jnp.float32), part_b + sums_b.astype(jnp.float32)
        with jax.named_scope(f"add{step}"):
            sums_a, sums_b = part_a.astype(jnp.bfloat16), part_b.astype(jnp.bfloat16)
    return jnp.concatenate([sums_a, sums_b], axis=0)


def prefix(part):
    gathered = lax.all_gather(part, AXIS)
    earlier = jnp.arange(gathered.shape[0]) < lax.axis_index(AXIS)
    return jnp.sum(jnp.where(earlier[:, None], gathered, 0), axis=0)


def exchange_form(tokens, expert_ids, gate_weights, weights_in, weights_out, placement, capacity):
    axis_len = lax.axis_size(AXIS)
    tok_rows, top_len = expert_ids.shape
    feat_len = tokens.shape[1]
    slot_len = tok_rows * top_len * 9 // (8 * axis_len)
    devices = jnp.arange(axis_len, dtype=jnp.int32)
    dev_of = jnp.sum(jnp.where(placement[:, None] == devices[None, :], devices[:, None], 0), axis=0)
    flat_ids = expert_ids.reshape(-1)
    onehot = (flat_ids[:, None] == devices[None, :]).astype(jnp.int32)
    before = jnp.cumsum(onehot, axis=0) - onehot
    local_rank = jnp.sum(before * onehot, axis=1)
    counts = jnp.sum(onehot, axis=0)
    offset = prefix(counts)
    row_offset = jnp.sum(onehot * offset[None, :], axis=1)
    row_cap = jnp.sum(onehot * capacity[None, :], axis=1)
    row_dest = jnp.sum(onehot * dev_of[None, :], axis=1)
    kept = local_rank + row_offset < row_cap
    flat_slot = row_dest * slot_len + local_rank
    row_token = jnp.arange(tok_rows * top_len, dtype=jnp.int32) // top_len
    owner = jnp.full((axis_len * slot_len,), tok_rows, jnp.int32).at[flat_slot].set(row_token)
    padded_tokens = jnp.concatenate([tokens, jnp.zeros((1, feat_len), jnp.bfloat16)], axis=0)
    outgoing = padded_tokens[owner].reshape(axis_len, slot_len, feat_len)
    arrived = lax.all_to_all(outgoing, AXIS, split_axis=0, concat_axis=0, tiled=True)
    items = arrived.shape[1]
    result_rows = expert_block(
        arrived.reshape(axis_len * items, feat_len), weights_in[0], weights_out[0]
    )
    result_rows = result_rows.reshape(axis_len, items, feat_len)
    returned = lax.all_to_all(result_rows, AXIS, split_axis=0, concat_axis=0, tiled=True)
    picked = returned.reshape(axis_len * slot_len, feat_len)[flat_slot]
    row_weight = jnp.where(kept, gate_weights.reshape(-1), jnp.float32(0.0))
    combined = jnp.sum(
        (row_weight[:, None] * picked.astype(jnp.float32)).reshape(tok_rows, top_len, feat_len),
        axis=1,
    )
    return combined.astype(jnp.bfloat16)


def local(*args):
    axis_len, top_len = lax.axis_size(AXIS), args[1].shape[1]
    dense = axis_len <= 2 * top_len and axis_len % 4 == 0
    return ring_form(*args) if dense else exchange_form(*args)


def solution(mesh):
    in_specs = (
        P(("group", "expert"), None),
        P(("group", "expert"), None),
        P(("group", "expert"), None),
        P(("group", "expert"), None, None),
        P(("group", "expert"), None, None),
        P("group"),
        P("group"),
    )
    out_specs = P(("group", "expert"), None)
    return jax.shard_map(local, mesh=mesh, in_specs=in_specs, out_specs=out_specs, check_vma=False)
```

```python
import jax
import jax.numpy as jnp
import numpy as np
from jax import lax
from jax.experimental import pallas as pl
from jax.experimental.pallas import tpu as pltpu
from jax.sharding import PartitionSpec as P

AXIS = "expert"
COST = pl.CostEstimate(flops=12_000_000_000, transcendentals=0, bytes_accessed=60_000_000)


def expert_block(inputs, first_weights, second_weights):
    hidden_len = first_weights.shape[1] // 2
    projected = jnp.dot(inputs, first_weights, preferred_element_type=jnp.float32)
    gate_part = projected[:, :hidden_len]
    up_part = projected[:, hidden_len:]
    hidden = (jax.nn.silu(gate_part) * up_part).astype(jnp.bfloat16)
    return jnp.dot(hidden, second_weights, preferred_element_type=jnp.float32).astype(jnp.bfloat16)


def incoming_gates(expert_ids, gate_weights, placement):
    named = expert_ids.T[None] == placement[:, None, None]
    outgoing = jnp.sum(jnp.where(named, gate_weights.T[None], 0.0), axis=1)
    return lax.all_to_all(outgoing[:, None], AXIS, split_axis=0, concat_axis=0, tiled=True)[:, 0]


def table_kernel(mine, placement, capacity, owners, gate_ref, *refs):
    limit = capacity[placement[mine[0]]]
    gate = gate_ref[...]
    devices, rows = gate.shape
    hit = jnp.where(gate > 0, 1.0, 0.0).astype(jnp.bfloat16)
    shape = (rows, rows)
    lower = lax.broadcasted_iota(jnp.int32, shape, 0) < lax.broadcasted_iota(jnp.int32, shape, 1)
    lower = jnp.where(lower, 1.0, 0.0).astype(jnp.bfloat16)
    within = jnp.dot(hit, lower, preferred_element_type=jnp.float32)
    shape = (devices, devices)
    earlier = lax.broadcasted_iota(jnp.int32, shape, 1) < lax.broadcasted_iota(jnp.int32, shape, 0)
    earlier = jnp.where(earlier, 1.0, 0.0).astype(jnp.bfloat16)
    before = jnp.dot(earlier, hit, preferred_element_type=jnp.float32)
    rank = within + jnp.sum(before, axis=1, keepdims=True)
    table = jnp.where(rank < limit.astype(jnp.float32), gate, 0.0).T
    out = refs[-1]
    steps = out.shape[1]
    half = rows // 2
    column = lax.broadcasted_iota(jnp.int32, (half, devices), 1)
    turn = lax.broadcasted_iota(jnp.int32, (half, steps), 1)
    for index in range(4):
        part = index % 2 * half
        piece = table[part : part + half]
        made = jnp.zeros((half, steps), jnp.float32)
        for step in range(steps):
            picked = jnp.sum(jnp.where(column == owners[(mine[0] * steps + step) * 4 + index], piece, 0.0), axis=1, keepdims=True)
            made = jnp.where(turn == step, picked, made)
        out[index * half : (index + 1) * half, :] = made


def weight_table(gate, owners, placement, capacity, gates):
    smem = pl.BlockSpec(memory_space=pltpu.SMEM)
    hbm = pl.BlockSpec(memory_space=pl.ANY)
    vmem = pl.BlockSpec(memory_space=pltpu.VMEM)
    mine = lax.axis_index(AXIS).astype(jnp.int32).reshape(1)
    return pl.pallas_call(
        table_kernel,
        out_shape=jax.ShapeDtypeStruct((2 * gate.shape[1], owners.shape[1]), jnp.float32),
        in_specs=[smem] * 4 + [vmem] + [hbm] * len(gates),
        out_specs=vmem,
        cost_estimate=COST,
    )(mine, placement, capacity, jnp.asarray(owners.reshape(-1)), gate, *gates)


def ring_form(tokens, expert_ids, gate_weights, weights_in, weights_out, placement, capacity):
    axis_len = lax.axis_size(AXIS)
    rows = tokens.shape[0]
    half = rows // 2
    chips = axis_len // 2
    side = chips // 2

    def chip_at(spot):
        return 2 * spot if spot < side else 2 * (chips - 1 - spot) + 1

    spot_of = {chip_at(spot): spot for spot in range(chips)}

    def along(step):
        return [(d, 2 * chip_at((spot_of[d // 2] + step) % chips) + d % 2) for d in range(axis_len)]

    forth, back = along(1), along(-1)
    swap = [(d, d ^ 1) for d in range(axis_len)]

    def send(value, where, name):
        with jax.named_scope(name):
            return lax.ppermute(value, AXIS, where)

    owners = np.zeros((axis_len, chips, 4), np.int32)
    for d in range(axis_len):
        for step in range(chips):
            for index, (way, core) in enumerate([(-1, 0), (1, 0), (-1, 1), (1, 1)]):
                owners[d, step, index] = 2 * chip_at((spot_of[d // 2] + way * step) % chips) + (d + core) % 2
    first_weights, second_weights = weights_in[0], weights_out[0]

    aheads, behinds = [tokens[:half]], [tokens[half:]]
    for step in range(1, chips):
        aheads.append(send(aheads[-1], forth, f"ag{step}a"))
        behinds.append(send(behinds[-1], back, f"ag{step}b"))
    with jax.named_scope("meta"):
        gate = incoming_gates(expert_ids, gate_weights, placement)
        scales = weight_table(gate, owners, placement, capacity, (aheads[1], behinds[1]))
    joined = min(3, chips - 1)
    sums_a = sums_b = None
    for turn in range(1, chips + 1):
        step = turn % chips
        pieces = [aheads[step], behinds[step]]
        if step:
            pieces += [send(pieces[0], swap, f"xs{step}a"), send(pieces[1], swap, f"xs{step}b")]
        with jax.named_scope(f"kernel{step}"):
            if step == joined:
                pieces += [tokens, send(tokens, swap, "xs0")]
            if step:
                outs = expert_block(jnp.concatenate(pieces, axis=0), first_weights, second_weights)
            else:
                outs = own_outs
            if step == joined:
                outs, own_outs = outs[: 2 * rows], outs[2 * rows :]
            outs = outs.astype(jnp.float32) * scales[:, step : step + 1]
            kept, other = outs[:rows], outs[rows:].astype(jnp.bfloat16)
        from_other = send(other, swap, f"ps{step}")
        with jax.named_scope(f"add{step}"):
            part = kept + from_other.astype(jnp.float32)
            part_a, part_b = part[:half], part[half:]
        if turn != 1:
            sums_a, sums_b = send(sums_a, forth, f"rs{step}a"), send(sums_b, back, f"rs{step}b")
            if step == 0:
                got = jnp.concatenate([sums_a, sums_b], axis=0)
                return (part + got.astype(jnp.float32)).astype(jnp.bfloat16)
            with jax.named_scope(f"add{step}"):
                part_a, part_b = part_a + sums_a.astype(jnp.float32), part_b + sums_b.astype(jnp.float32)
        with jax.named_scope(f"add{step}"):
            sums_a, sums_b = part_a.astype(jnp.bfloat16), part_b.astype(jnp.bfloat16)


def prefix(part):
    gathered = lax.all_gather(part, AXIS)
    earlier = jnp.arange(gathered.shape[0]) < lax.axis_index(AXIS)
    return jnp.sum(jnp.where(earlier[:, None], gathered, 0), axis=0)


def exchange_form(tokens, expert_ids, gate_weights, weights_in, weights_out, placement, capacity):
    axis_len = lax.axis_size(AXIS)
    tok_rows, top_len = expert_ids.shape
    feat_len = tokens.shape[1]
    slot_len = tok_rows * top_len * 9 // (8 * axis_len)
    devices = jnp.arange(axis_len, dtype=jnp.int32)
    dev_of = jnp.sum(jnp.where(placement[:, None] == devices[None, :], devices[:, None], 0), axis=0)
    flat_ids = expert_ids.reshape(-1)
    onehot = (flat_ids[:, None] == devices[None, :]).astype(jnp.int32)
    before = jnp.cumsum(onehot, axis=0) - onehot
    local_rank = jnp.sum(before * onehot, axis=1)
    counts = jnp.sum(onehot, axis=0)
    offset = prefix(counts)
    row_offset = jnp.sum(onehot * offset[None, :], axis=1)
    row_cap = jnp.sum(onehot * capacity[None, :], axis=1)
    row_dest = jnp.sum(onehot * dev_of[None, :], axis=1)
    kept = local_rank + row_offset < row_cap
    flat_slot = row_dest * slot_len + local_rank
    row_token = jnp.arange(tok_rows * top_len, dtype=jnp.int32) // top_len
    owner = jnp.full((axis_len * slot_len,), tok_rows, jnp.int32).at[flat_slot].set(row_token)
    padded_tokens = jnp.concatenate([tokens, jnp.zeros((1, feat_len), jnp.bfloat16)], axis=0)
    outgoing = padded_tokens[owner].reshape(axis_len, slot_len, feat_len)
    arrived = lax.all_to_all(outgoing, AXIS, split_axis=0, concat_axis=0, tiled=True)
    items = arrived.shape[1]
    result_rows = expert_block(
        arrived.reshape(axis_len * items, feat_len), weights_in[0], weights_out[0]
    )
    result_rows = result_rows.reshape(axis_len, items, feat_len)
    returned = lax.all_to_all(result_rows, AXIS, split_axis=0, concat_axis=0, tiled=True)
    picked = returned.reshape(axis_len * slot_len, feat_len)[flat_slot]
    row_weight = jnp.where(kept, gate_weights.reshape(-1), jnp.float32(0.0))
    combined = jnp.sum(
        (row_weight[:, None] * picked.astype(jnp.float32)).reshape(tok_rows, top_len, feat_len),
        axis=1,
    )
    return combined.astype(jnp.bfloat16)


def local(*args):
    axis_len, top_len = lax.axis_size(AXIS), args[1].shape[1]
    dense = axis_len <= 2 * top_len and axis_len % 4 == 0
    return ring_form(*args) if dense else exchange_form(*args)


def solution(mesh):
    in_specs = (
        P(("group", "expert"), None),
        P(("group", "expert"), None),
        P(("group", "expert"), None),
        P(("group", "expert"), None, None),
        P(("group", "expert"), None, None),
        P("group"),
        P("group"),
    )
    out_specs = P(("group", "expert"), None)
    return jax.shard_map(local, mesh=mesh, in_specs=in_specs, out_specs=out_specs, check_vma=False)
```
